32 devices in a mesh: groups: 2 (over y), rows: 4 (over z), feat: 4 (over x, core).
Axes of the slice: x: 2, y: 2, z: 4, core: 2. Of those that a mesh axis runs over, the one named last changes fastest.
Arguments:
- student: float32 [1280, 4096], P(('groups', 'rows'), 'feat'), parts along dimension 0, may hold values from -1 to 1
- teacher: bfloat16 [1280, 1024], P(('groups', 'rows'), 'feat'), parts along dimension 0, may hold values from -1 to 1
Outputs:
- row_loss: float32 [1280], P(('groups', 'rows')), parts along dimension 0
- student_grad: float32 [1280, 4096], P(('groups', 'rows'), 'feat'), parts along dimension 0
The draws below stay inside these ranges and needn't reach their ends.
There are 2 independent parts, one for each index of `groups`. The reference program is written for one: setup_inputs(seed, part) draws one part's arguments, and reference() takes and returns one part's arrays. A program takes and returns all parts, laid end to end along the dimension named above; each array names one. Nothing has to cross between parts.
All inputs are finite; a program needn't handle non-finite values.
Results may differ from the reference program's by a relative error of at most 0.0085.
Values may be sent and summed in bfloat16 or wider, within the bound.
A program may use at most 64 MiB of HBM per device.

```python
import math
import jax
import jax.numpy as jnp
from jax import lax

D = 4096
DT = 1024
EMBEDS = 640
N_FEAT = 4


def draw_student(key, part):
    keys = jax.random.split(jax.random.fold_in(key, 11), 3)
    row_scale = jnp.exp(jax.random.uniform(keys[0], (EMBEDS, 1), jnp.float32) * math.log(10.0))
    col_scale = jnp.exp(jax.random.uniform(keys[1], (1, D), jnp.float32) * math.log(10.0))
    base = jnp.clip(jax.random.normal(keys[2], (EMBEDS, D), jnp.float32), -4.0, 4.0)
    return (base * row_scale * col_scale * (0.02 / math.sqrt(D))).astype(jnp.float32)


def draw_teacher(key, part):
    keys = jax.random.split(jax.random.fold_in(key, 23), 1)
    base = jnp.clip(jax.random.normal(keys[0], (EMBEDS, DT), jnp.float32), -4.0, 4.0)
    return (base / math.sqrt(DT)).astype(jnp.bfloat16)


def setup_inputs(seed: int = 0, part: int = 0) -> dict:
    splits = jax.random.split(jax.random.key(seed), 3)
    part_splits = jax.random.split(jax.random.fold_in(splits[2], part), 3)
    student = draw_student(jax.random.fold_in(jax.random.fold_in(splits[2], part), 71), part)
    teacher = draw_teacher(jax.random.fold_in(jax.random.fold_in(splits[2], part), 71), part)
    return dict(student=student, teacher=teacher)


EPSILON = 1e-06

def reference(student, teacher):
    squares = lax.optimization_barrier(jnp.sum(student * student, axis=1))
    scaling = lax.rsqrt(squares + EPSILON)
    unit = student * scaling[:, None]
    unit_half = unit.astype(jnp.bfloat16)
    slice_width = D // N_FEAT
    teach_width = DT // N_FEAT
    block_rows = math.gcd(512, EMBEDS)
    contract = (((1,), (1,)), ((), ()))

    def one_block(start):
        mine = lax.dynamic_slice_in_dim(unit_half, start, block_rows, 0)
        mine_teacher = lax.dynamic_slice_in_dim(teacher, start, block_rows, 0)
        differ = jnp.zeros((block_rows, EMBEDS), jnp.float32)
        for feature_slice in range(N_FEAT):
            lower = feature_slice * slice_width
            upper = lower + slice_width
            tlower = feature_slice * teach_width
            tupper = tlower + teach_width
            student_term = lax.dot_general(mine[:, lower:upper], unit_half[:, lower:upper], contract, preferred_element_type=jnp.float32)
            teacher_term = lax.dot_general(mine_teacher[:, tlower:tupper], teacher[:, tlower:tupper], contract, preferred_element_type=jnp.float32)
            term = lax.optimization_barrier((student_term - teacher_term).astype(jnp.bfloat16)).astype(jnp.float32)
            differ = differ + term
        losses = lax.optimization_barrier(jnp.sum(differ * differ, axis=1))
        pulled = jnp.dot(differ.astype(jnp.bfloat16), unit_half, preferred_element_type=jnp.float32)
        return (losses, pulled)
    starts = jnp.arange(EMBEDS // block_rows, dtype=jnp.int32) * block_rows
    losses, pulled = lax.map(one_block, starts)
    losses = losses.reshape(EMBEDS)
    pulled = pulled.reshape(EMBEDS, D)
    radial = lax.optimization_barrier(jnp.sum(pulled * unit, axis=1))
    factor = 4.0 * D / EMBEDS
    student_grad = factor * scaling[:, None] * (pulled - radial[:, None] * unit)
    return (D / EMBEDS * losses, student_grad)
```

```python
import functools

import jax
import jax.numpy as jnp
from jax import lax
from jax.experimental import pallas as pl
from jax.experimental.pallas import tpu as pltpu
from jax.sharding import PartitionSpec as P

D = 4096
EPSILON = 1e-06
ROWS_LIMIT = 8
LAST = (((1,), (1,)), ((), ()))
FIRST = (((0,), (0,)), ((), ()))
F32 = jnp.float32
BF16 = jnp.bfloat16
MESH = pl.DeviceIdType.MESH


def shifted(block, axis, distance):
    devices = range(lax.axis_size(axis))
    route = [((i - distance) % len(devices), i) for i in devices]
    return lax.ppermute(block, axis, route)


def ring(student, teacher):
    cycle = lax.axis_size("rows")
    rows_here = student.shape[0]
    width = student.shape[1]
    embeds = rows_here * cycle
    squares = lax.psum(jnp.sum(student * student, axis=1), "feat")
    scaling = lax.rsqrt(squares + EPSILON)
    unit = student * scaling[:, None]
    unit_half = unit.astype(BF16)
    packed = jnp.concatenate([unit_half, teacher], axis=1)

    def absorb(carry, visitor):
        losses, pulled = carry
        other_unit = visitor[:, :width]
        other_teacher = visitor[:, width:]
        student_term = lax.dot_general(
            unit_half, other_unit, LAST, preferred_element_type=F32
        )
        teacher_term = lax.dot_general(
            teacher, other_teacher, LAST, preferred_element_type=F32
        )
        differ = lax.psum((student_term - teacher_term).astype(BF16), "feat").astype(F32)
        losses = losses + jnp.sum(differ * differ, axis=1)
        pulled = pulled + jnp.dot(
            differ.astype(BF16), other_unit, preferred_element_type=F32
        )
        return (losses, pulled)

    carry = (jnp.zeros((rows_here,), F32), jnp.zeros((rows_here, width), F32))
    carry = absorb(carry, packed)

    def turn(step, state):
        inner, visitor = state
        visitor = shifted(visitor, "rows", 1)
        return (absorb(inner, visitor), visitor)

    carry, visitor = lax.fori_loop(0, cycle - 1, turn, (carry, packed))
    losses, pulled = carry
    radial = lax.psum(jnp.sum(pulled * unit, axis=1), "feat")
    factor = 4.0 * D / embeds
    student_grad = factor * scaling[:, None] * (pulled - radial[:, None] * unit)
    return (D / embeds * losses, student_grad)


def kernel(
    R, F, C, x_ref, t_ref, loss_ref, g_ref,
    U, T, SQ, CX, TX, rad_ref,
    us, ur, ts, tr, qs, qr, cs, cr, xs, xr,
):
    z = lax.axis_index("rows")
    f = lax.axis_index("feat")
    n, w = x_ref.shape
    rc = n // C
    not_low = z > 0
    not_high = z < R - 1

    bar = pltpu.get_barrier_semaphore()
    for p in range(1, F):
        pl.semaphore_signal(
            bar, inc=1, device_id={"feat": lax.rem(f + p, F)}, device_id_type=MESH
        )

    @pl.when(not_low)
    def _():
        pl.semaphore_signal(bar, inc=1, device_id={"rows": z - 1}, device_id_type=MESH)

    @pl.when(not_high)
    def _():
        pl.semaphore_signal(bar, inc=1, device_id={"rows": z + 1}, device_id_type=MESH)

    eye = lax.broadcasted_iota(jnp.int32, (n, n), 0) == lax.broadcasted_iota(
        jnp.int32, (n, n), 1
    )

    def to_row(column):
        return jnp.sum(jnp.where(eye, column, 0.0), axis=0, keepdims=True)

    def to_column(row):
        return jnp.sum(jnp.where(eye, row, 0.0), axis=1, keepdims=True)

    x = x_ref[...]
    SQ[f] = jnp.broadcast_to(to_row(jnp.sum(x * x, axis=1, keepdims=True)), (8, n))
    T[z] = t_ref[...]
    pl.semaphore_wait(
        bar, F - 1 + not_low.astype(jnp.int32) + not_high.astype(jnp.int32)
    )

    def across(buf, index, send, recv, p, mine):
        owner = f if mine else lax.rem(f + F - p, F)
        ref = buf.at[(owner,) + index]
        return pltpu.make_async_remote_copy(
            src_ref=ref, dst_ref=ref,
            send_sem=send.at[index + (p - 1,)], recv_sem=recv.at[index + (p - 1,)],
            device_id={"feat": lax.rem(f + p, F)}, device_id_type=MESH,
        )

    def spread(buf, index, send, recv):
        for p in range(1, F):
            across(buf, index, send, recv, p, True).start()

    def collect(buf, index, send, recv):
        for p in range(1, F):
            across(buf, index, send, recv, p, False).wait_recv()

    def drained(buf, index, send, recv):
        for p in range(1, F):
            across(buf, index, send, recv, p, True).wait_send()

    def along(buf, d, src, place, index, send, recv):
        ref = buf.at[(src,) + place]
        target = lax.rem(z + (1 if d == 0 else R - 1), R)
        return pltpu.make_async_remote_copy(
            src_ref=ref, dst_ref=ref,
            send_sem=send.at[(d,) + index], recv_sem=recv.at[(d,) + index],
            device_id={"rows": target}, device_id_type=MESH,
        )

    def sends(d, k):
        if d == 0:
            return jnp.logical_and(z - k >= 0, not_high), z - k
        return jnp.logical_and(z + k <= R - 1, not_low), z + k

    def arrives(d, k):
        if d == 0:
            return z - 1 - k >= 0, z - 1 - k
        return z + 1 + k <= R - 1, z + 1 + k

    def t_copy(d, k, src):
        return along(T, d, src, (), (k,), ts, tr)

    def u_copy(d, k, c, src):
        return along(U, d, src, (c,), (k, c), us, ur)

    spread(SQ, (), qs, qr)
    for d in range(2):
        here, src = sends(d, 0)

        @pl.when(here)
        def _(d=d, src=src):
            t_copy(d, 0, src).start()

    collect(SQ, (), qs, qr)
    squares = SQ[0]
    for g in range(1, F):
        squares = squares + SQ[g]
    scaling = to_column(lax.rsqrt(squares[:1] + EPSILON))
    U[z] = (x_ref[...] * scaling).astype(BF16).reshape(C, rc, w)
    for c in range(C):
        for d in range(2):
            here, src = sends(d, 0)

            @pl.when(here)
            def _(d=d, c=c, src=src):
                u_copy(d, 0, c, src).start()

    def teach(src):
        TX[f, src] = lax.dot_general(
            T[src], t_ref[...], LAST, preferred_element_type=F32
        ).astype(BF16)
        spread(TX, (src,), xs, xr)

    def study(src, c):
        CX[f, src, c] = lax.dot_general(
            U[src, c], U[z].reshape(n, w), LAST, preferred_element_type=F32
        ).astype(BF16)
        spread(CX, (src, c), cs, cr)

    def finish(src, first=False):
        collect(TX, (src,), xs, xr)
        teacher = TX[0, src].astype(F32)
        for g in range(1, F):
            teacher = teacher + TX[g, src].astype(F32)
        for c in range(C):
            collect(CX, (src, c), cs, cr)
        cosine = CX[0, src].astype(F32)
        for g in range(1, F):
            cosine = cosine + CX[g, src].astype(F32)
        cosine = cosine.reshape(n, n)
        differ = cosine - teacher
        half = differ.astype(BF16)
        loss = jnp.sum(differ * differ, axis=0, keepdims=True)
        radial = jnp.sum(half.astype(F32) * cosine, axis=0, keepdims=True)
        pulled = lax.dot_general(
            half, U[src].reshape(n, w), FIRST, preferred_element_type=F32
        )
        if first:
            loss_ref[...] = loss
            rad_ref[...] = radial
            g_ref[...] = pulled
        else:
            loss_ref[...] += loss
            rad_ref[...] += radial
            g_ref[...] += pulled

    teach(z)
    for c in range(C):
        study(z, c)

    for k in range(R - 1):
        for d in range(2):
            here, src = arrives(d, k)

            @pl.when(here)
            def _(d=d, k=k, src=src):
                t_copy(d, k, src).wait_recv()
                if k < R - 2:
                    @pl.when(sends(d, k + 1)[0])
                    def _():
                        t_copy(d, k + 1, src).start()
                teach(src)

        if k == 0:
            finish(z, True)
        else:
            for d in range(2):
                here, src = arrives(d, k - 1)

                @pl.when(here)
                def _(src=src):
                    finish(src)

        for c in range(C):
            for d in range(2):
                here, src = arrives(d, k)

                @pl.when(here)
                def _(d=d, k=k, c=c, src=src):
                    u_copy(d, k, c, src).wait_recv()
                    if k < R - 2:
                        @pl.when(sends(d, k + 1)[0])
                        def _():
                            u_copy(d, k + 1, c, src).start()
                    study(src, c)

    for d in range(2):
        here, src = arrives(d, R - 2)

        @pl.when(here)
        def _(src=src):
            finish(src)

    factor = 4.0 * D / (n * R)
    loss_ref[...] = (D / (n * R)) * loss_ref[...]
    radial = to_column(rad_ref[...])
    g_ref[...] = (factor * scaling) * (g_ref[...] - (radial * scaling) * x_ref[...])

    drained(SQ, (), qs, qr)
    for src in range(R):
        drained(TX, (src,), xs, xr)
        for c in range(C):
            drained(CX, (src, c), cs, cr)
    for k in range(R - 1):
        for d in range(2):
            here, src = sends(d, k)

            @pl.when(here)
            def _(d=d, k=k, src=src):
                t_copy(d, k, src).wait_send()
                for c in range(C):
                    u_copy(d, k, c, src).wait_send()


def fused(R, F, student, teacher):
    n, w = student.shape
    wt = teacher.shape[1]
    C = 2 if n % 32 == 0 else 1
    dma = pltpu.SemaphoreType.DMA
    vmem = pl.BlockSpec(memory_space=pltpu.VMEM)
    loss, grad = pl.pallas_call(
        functools.partial(kernel, R, F, C),
        out_shape=(
            jax.ShapeDtypeStruct((1, n), F32),
            jax.ShapeDtypeStruct((n, w), F32),
        ),
        in_specs=[vmem, vmem],
        out_specs=(vmem, vmem),
        scratch_shapes=[
            pltpu.VMEM((R, C, n // C, w), BF16),
            pltpu.VMEM((R, n, wt), BF16),
            pltpu.VMEM((F, 8, n), F32),
            pltpu.VMEM((F, R, C, n // C, n), BF16),
            pltpu.VMEM((F, R, n, n), BF16),
            pltpu.VMEM((1, n), F32),
            dma((2, R - 1, C)), dma((2, R - 1, C)),
            dma((2, R - 1)), dma((2, R - 1)),
            dma((F - 1,)), dma((F - 1,)),
            dma((R, C, F - 1)), dma((R, C, F - 1)),
            dma((R, F - 1)), dma((R, F - 1)),
        ],
        compiler_params=pltpu.CompilerParams(
            collective_id=0, has_side_effects=True, vmem_limit_bytes=40 * 2**20
        ),
    )(student, teacher)
    return loss.reshape(n), grad


def solution(mesh):
    R, F = mesh.shape["rows"], mesh.shape["feat"]
    body = functools.partial(fused, R, F) if 2 <= R <= ROWS_LIMIT and F > 1 else ring
    in_specs = (P(("groups", "rows"), "feat"), P(("groups", "rows"), "feat"))
    out_specs = (P(("groups", "rows")), P(("groups", "rows"), "feat"))
    return jax.shard_map(
        body, mesh=mesh, in_specs=in_specs, out_specs=out_specs, check_vma=False
    )
```

```python
import functools

import jax
import jax.numpy as jnp
from jax import lax
from jax.experimental import pallas as pl
from jax.experimental.pallas import tpu as pltpu
from jax.sharding import PartitionSpec as P

D = 4096
EPSILON = 1e-06
ROWS_LIMIT = 8
LAST = (((1,), (1,)), ((), ()))
FIRST = (((0,), (0,)), ((), ()))
F32 = jnp.float32
BF16 = jnp.bfloat16
MESH = pl.DeviceIdType.MESH


def shifted(block, axis, distance):
    devices = range(lax.axis_size(axis))
    route = [((i - distance) % len(devices), i) for i in devices]
    return lax.ppermute(block, axis, route)


def ring(student, teacher):
    cycle = lax.axis_size("rows")
    rows_here = student.shape[0]
    width = student.shape[1]
    embeds = rows_here * cycle
    squares = lax.psum(jnp.sum(student * student, axis=1), "feat")
    scaling = lax.rsqrt(squares + EPSILON)
    unit = student * scaling[:, None]
    unit_half = unit.astype(BF16)
    packed = jnp.concatenate([unit_half, teacher], axis=1)

    def absorb(carry, visitor):
        losses, pulled = carry
        other_unit = visitor[:, :width]
        other_teacher = visitor[:, width:]
        student_term = lax.dot_general(
            unit_half, other_unit, LAST, preferred_element_type=F32
        )
        teacher_term = lax.dot_general(
            teacher, other_teacher, LAST, preferred_element_type=F32
        )
        differ = lax.psum((student_term - teacher_term).astype(BF16), "feat").astype(F32)
        losses = losses + jnp.sum(differ * differ, axis=1)
        pulled = pulled + jnp.dot(
            differ.astype(BF16), other_unit, preferred_element_type=F32
        )
        return (losses, pulled)

    carry = (jnp.zeros((rows_here,), F32), jnp.zeros((rows_here, width), F32))
    carry = absorb(carry, packed)

    def turn(step, state):
        inner, visitor = state
        visitor = shifted(visitor, "rows", 1)
        return (absorb(inner, visitor), visitor)

    carry, visitor = lax.fori_loop(0, cycle - 1, turn, (carry, packed))
    losses, pulled = carry
    radial = lax.psum(jnp.sum(pulled * unit, axis=1), "feat")
    factor = 4.0 * D / embeds
    student_grad = factor * scaling[:, None] * (pulled - radial[:, None] * unit)
    return (D / embeds * losses, student_grad)


def kernel(
    R, F, C, x_hbm, t_hbm, loss_ref, g_ref,
    x_ref, t_ref, U, T, SQ, TP, TQ, TX, CP, CQ, CX, DX, rad_ref,
    ins, us, ur, ts, tr, qs, qr, tps, tpr, txs, txr, cps, cpr, cxs, cxr, dxs, dxr,
):
    z = lax.axis_index("rows")
    f = lax.axis_index("feat")
    core = lax.rem(f, 2)
    chip = lax.div(f, 2)
    n, w = x_ref.shape
    h = n // 2
    rc = n // C
    not_low = z > 0
    not_high = z < R - 1

    bar = pltpu.get_barrier_semaphore()
    for p in range(1, F):
        pl.semaphore_signal(
            bar, inc=1, device_id={"feat": lax.rem(f + p, F)}, device_id_type=MESH
        )

    @pl.when(not_low)
    def _():
        pl.semaphore_signal(bar, inc=1, device_id={"rows": z - 1}, device_id_type=MESH)

    @pl.when(not_high)
    def _():
        pl.semaphore_signal(bar, inc=1, device_id={"rows": z + 1}, device_id_type=MESH)

    x_in = pltpu.make_async_copy(x_hbm, x_ref, ins.at[0])
    t_in = pltpu.make_async_copy(t_hbm, t_ref, ins.at[1])
    x_in.start()
    t_in.start()

    eye = lax.broadcasted_iota(jnp.int32, (n, n), 0) == lax.broadcasted_iota(
        jnp.int32, (n, n), 1
    )

    def to_row(column):
        return jnp.sum(jnp.where(eye, column, 0.0), axis=0, keepdims=True)

    def to_column(row):
        return jnp.sum(jnp.where(eye, row, 0.0), axis=1, keepdims=True)

    x_in.wait()
    x = x_ref[...]
    SQ[f] = jnp.broadcast_to(to_row(jnp.sum(x * x, axis=1, keepdims=True)), (8, n))
    t_in.wait()
    T[z] = t_ref[...]
    pl.semaphore_wait(
        bar, F - 1 + not_low.astype(jnp.int32) + not_high.astype(jnp.int32)
    )

    def remote(src, dst, send, recv, device):
        return pltpu.make_async_remote_copy(
            src_ref=src, dst_ref=dst, send_sem=send, recv_sem=recv,
            device_id=device, device_id_type=MESH,
        )

    def across(entry, index, send, recv, p, mine):
        ref = entry(f if mine else lax.rem(f + F - p, F))
        return remote(
            ref, ref, send.at[index + (p - 1,)], recv.at[index + (p - 1,)],
            {"feat": lax.rem(f + p, F)},
        )

    def spread(entry, index, send, recv):
        for p in range(1, F):
            across(entry, index, send, recv, p, True).start()

    def collect(entry, index, send, recv):
        for p in range(1, F):
            across(entry, index, send, recv, p, False).wait_recv()

    def drained(entry, index, send, recv):
        for p in range(1, F):
            across(entry, index, send, recv, p, True).wait_send()

    def halves(buf, src):
        return lambda g: buf.at[lax.div(g, 2), src, lax.rem(g, 2)]

    def sibling(part, other, src, send, recv):
        return remote(
            part.at[src, 1 - core], other.at[src], send.at[src], recv.at[src],
            {"feat": f + 1 - 2 * core},
        )

    def along(buf, d, src, place, index, send, recv):
        ref = buf.at[(src,) + place]
        target = lax.rem(z + (1 if d == 0 else R - 1), R)
        return remote(
            ref, ref, send.at[(d,) + index], recv.at[(d,) + index], {"rows": target}
        )

    def sends(d, k):
        if d == 0:
            return jnp.logical_and(z - k >= 0, not_high), z - k
        return jnp.logical_and(z + k <= R - 1, not_low), z + k

    def arrives(d, k):
        if d == 0:
            return z - 1 - k >= 0, z - 1 - k
        return z + 1 + k <= R - 1, z + 1 + k

    def each(k, act):
        for d in range(2):
            here, src = arrives(d, k)

            @pl.when(here)
            def _(d=d, src=src):
                act(d, src)

    def t_copy(d, k, src):
        return along(T, d, src, (), (k,), ts, tr)

    def u_copy(d, k, c, src):
        return along(U, d, src, (c,), (k, c), us, ur)

    squares_of = lambda g: SQ.at[g]
    spread(squares_of, (), qs, qr)
    for d in range(2):
        here, src = sends(d, 0)

        @pl.when(here)
        def _(d=d, src=src):
            t_copy(d, 0, src).start()

    collect(squares_of, (), qs, qr)
    squares = SQ[0]
    for g in range(1, F):
        squares = squares + SQ[g]
    scaling = to_column(lax.rsqrt(squares[:1] + EPSILON))
    U[z] = (x_ref[...] * scaling).astype(BF16).reshape(C, rc, w)
    for c in range(C):
        for d in range(2):
            here, src = sends(d, 0)

            @pl.when(here)
            def _(d=d, c=c, src=src):
                u_copy(d, 0, c, src).start()

    def teach(src):
        TP[src] = lax.dot_general(
            T[src], t_ref[...], LAST, preferred_element_type=F32
        ).astype(BF16).reshape(2, h, n)
        sibling(TP, TQ, src, tps, tpr).start()

    def teach_on(src):
        sibling(TP, TQ, src, tps, tpr).wait_recv()
        TX[chip, src, core] = (TP[src, core].astype(F32) + TQ[src].astype(F32)).astype(BF16)
        spread(halves(TX, src), (src,), txs, txr)

    def gram(src, c):
        return lax.dot_general(
            U[src, c], U[z].reshape(n, w), LAST, preferred_element_type=F32
        ).astype(BF16)

    def study(src, c):
        CP[src, c] = gram(src, c)
        if c == C - 1:
            sibling(CP, CQ, src, cps, cpr).start()

    def study_on(src):
        sibling(CP, CQ, src, cps, cpr).wait_recv()
        CX[chip, src, core] = (CP[src, core].astype(F32) + CQ[src].astype(F32)).astype(BF16)
        spread(halves(CX, src), (src,), cxs, cxr)

    def direct_of(c):
        return lambda g: DX.at[g, c]

    def study_direct(src, c):
        DX[f, c] = gram(src, c)
        spread(direct_of(c), (c,), dxs, dxr)

    def finish(src, first=False, direct=False):
        collect(halves(TX, src), (src,), txs, txr)
        teacher = TX[0, src].astype(F32) + TX[1, src].astype(F32)
        if direct:
            for c in range(C):
                collect(direct_of(c), (c,), dxs, dxr)
            cosine = DX[0].astype(F32)
            for g in range(1, F):
                cosine = cosine + DX[g].astype(F32)
        else:
            collect(halves(CX, src), (src,), cxs, cxr)
            cosine = CX[0, src].astype(F32) + CX[1, src].astype(F32)
        cosine = cosine.reshape(n, n)
        differ = cosine - teacher.reshape(n, n)
        half = differ.astype(BF16)
        loss = jnp.sum(differ * differ, axis=0, keepdims=True)
        radial = jnp.sum(half.astype(F32) * cosine, axis=0, keepdims=True)
        pulled = lax.dot_general(
            half, U[src].reshape(n, w), FIRST, preferred_element_type=F32
        )
        if first:
            loss_ref[...] = loss
            rad_ref[...] = radial
            g_ref[...] = pulled
        else:
            loss_ref[...] += loss
            rad_ref[...] += radial
            g_ref[...] += pulled

    teach(z)
    for c in range(C):
        study(z, c)
    teach_on(z)
    study_on(z)

    for k in range(R - 1):
        last = k == R - 2

        def t_step(d, src, k=k):
            t_copy(d, k, src).wait_recv()
            if k < R - 2:
                @pl.when(sends(d, k + 1)[0])
                def _():
                    t_copy(d, k + 1, src).start()
            teach(src)

        each(k, t_step)
        if k > 0:
            each(k - 1, lambda d, src: study_on(src))
        each(k, lambda d, src: teach_on(src))
        for c in range(C):

            def u_step(d, src, k=k, c=c, last=last):
                u_copy(d, k, c, src).wait_recv()
                if not last:
                    @pl.when(sends(d, k + 1)[0])
                    def _():
                        u_copy(d, k + 1, c, src).start()
                if last:
                    study_direct(src, c)
                else:
                    study(src, c)

            each(k, u_step)
            if c == 0:
                if k == 0:
                    finish(z, first=True)
                else:
                    each(k - 1, lambda d, src: finish(src))

    each(R - 2, lambda d, src: finish(src, direct=True))

    factor = 4.0 * D / (n * R)
    loss_ref[...] = (D / (n * R)) * loss_ref[...]
    radial = to_column(rad_ref[...])
    g_ref[...] = (factor * scaling) * (g_ref[...] - (radial * scaling) * x_ref[...])

    drained(squares_of, (), qs, qr)

    def t_drained(d, src):
        sibling(TP, TQ, src, tps, tpr).wait_send()
        drained(halves(TX, src), (src,), txs, txr)

    def c_drained(d, src):
        sibling(CP, CQ, src, cps, cpr).wait_send()
        drained(halves(CX, src), (src,), cxs, cxr)

    t_drained(0, z)
    c_drained(0, z)
    for k in range(R - 1):
        each(k, t_drained)
        if k < R - 2:
            each(k, c_drained)
        else:
            each(k, lambda d, src: [drained(direct_of(c), (c,), dxs, dxr) for c in range(C)])
        for d in range(2):
            here, src = sends(d, k)

            @pl.when(here)
            def _(d=d, k=k, src=src):
                t_copy(d, k, src).wait_send()
                for c in range(C):
                    u_copy(d, k, c, src).wait_send()


def fused(R, F, student, teacher):
    n, w = student.shape
    wt = teacher.shape[1]
    C = 2
    h = n // 2
    dma = pltpu.SemaphoreType.DMA
    vmem = pl.BlockSpec(memory_space=pltpu.VMEM)
    hbm = pl.BlockSpec(memory_space=pltpu.HBM)
    loss, grad = pl.pallas_call(
        functools.partial(kernel, R, F, C),
        out_shape=(
            jax.ShapeDtypeStruct((1, n), F32),
            jax.ShapeDtypeStruct((n, w), F32),
        ),
        in_specs=[hbm, hbm],
        out_specs=(vmem, vmem),
        scratch_shapes=[
            pltpu.VMEM((n, w), F32),
            pltpu.VMEM((n, wt), BF16),
            pltpu.VMEM((R, C, n // C, w), BF16),
            pltpu.VMEM((R, n, wt), BF16),
            pltpu.VMEM((F, 8, n), F32),
            pltpu.VMEM((R, 2, h, n), BF16),
            pltpu.VMEM((R, h, n), BF16),
            pltpu.VMEM((2, R, 2, h, n), BF16),
            pltpu.VMEM((R, 2, h, n), BF16),
            pltpu.VMEM((R, h, n), BF16),
            pltpu.VMEM((2, R, 2, h, n), BF16),
            pltpu.VMEM((F, C, n // C, n), BF16),
            pltpu.VMEM((1, n), F32),
            dma((2,)),
            dma((2, R - 1, C)), dma((2, R - 1, C)),
            dma((2, R - 1)), dma((2, R - 1)),
            dma((F - 1,)), dma((F - 1,)),
            dma((R,)), dma((R,)), dma((R, F - 1)), dma((R, F - 1)),
            dma((R,)), dma((R,)), dma((R, F - 1)), dma((R, F - 1)),
            dma((C, F - 1)), dma((C, F - 1)),
        ],
        compiler_params=pltpu.CompilerParams(
            collective_id=0, has_side_effects=True, vmem_limit_bytes=48 * 2**20
        ),
    )(student, teacher)
    return loss.reshape(n), grad


def solution(mesh):
    R, F = mesh.shape["rows"], mesh.shape["feat"]
    body = functools.partial(fused, R, F) if 2 <= R <= ROWS_LIMIT and F == 4 else ring
    in_specs = (P(("groups", "rows"), "feat"), P(("groups", "rows"), "feat"))
    out_specs = (P(("groups", "rows")), P(("groups", "rows"), "feat"))
    return jax.shard_map(
        body, mesh=mesh, in_specs=in_specs, out_specs=out_specs, check_vma=False
    )
```

```python
import functools

import jax
import jax.numpy as jnp
from jax import lax
from jax.experimental import pallas as pl
from jax.experimental.pallas import tpu as pltpu
from jax.sharding import PartitionSpec as P

D = 4096
EPSILON = 1e-06
ROWS_LIMIT = 8
LAST = (((1,), (1,)), ((), ()))
FIRST = (((0,), (0,)), ((), ()))
F32 = jnp.float32
BF16 = jnp.bfloat16
MESH = pl.DeviceIdType.MESH


def shifted(block, axis, distance):
    devices = range(lax.axis_size(axis))
    route = [((i - distance) % len(devices), i) for i in devices]
    return lax.ppermute(block, axis, route)


def ring(student, teacher):
    cycle = lax.axis_size("rows")
    rows_here = student.shape[0]
    width = student.shape[1]
    embeds = rows_here * cycle
    squares = lax.psum(jnp.sum(student * student, axis=1), "feat")
    scaling = lax.rsqrt(squares + EPSILON)
    unit = student * scaling[:, None]
    unit_half = unit.astype(BF16)
    packed = jnp.concatenate([unit_half, teacher], axis=1)

    def absorb(carry, visitor):
        losses, pulled = carry
        other_unit = visitor[:, :width]
        other_teacher = visitor[:, width:]
        student_term = lax.dot_general(
            unit_half, other_unit, LAST, preferred_element_type=F32
        )
        teacher_term = lax.dot_general(
            teacher, other_teacher, LAST, preferred_element_type=F32
        )
        differ = lax.psum((student_term - teacher_term).astype(BF16), "feat").astype(F32)
        losses = losses + jnp.sum(differ * differ, axis=1)
        pulled = pulled + jnp.dot(
            differ.astype(BF16), other_unit, preferred_element_type=F32
        )
        return (losses, pulled)

    carry = (jnp.zeros((rows_here,), F32), jnp.zeros((rows_here, width), F32))
    carry = absorb(carry, packed)

    def turn(step, state):
        inner, visitor = state
        visitor = shifted(visitor, "rows", 1)
        return (absorb(inner, visitor), visitor)

    carry, visitor = lax.fori_loop(0, cycle - 1, turn, (carry, packed))
    losses, pulled = carry
    radial = lax.psum(jnp.sum(pulled * unit, axis=1), "feat")
    factor = 4.0 * D / embeds
    student_grad = factor * scaling[:, None] * (pulled - radial[:, None] * unit)
    return (D / embeds * losses, student_grad)


def kernel(
    R, F, C, x_hbm, t_hbm, loss_ref, g_ref,
    x_ref, t_ref, U, T, SQ, TP, TQ, TX, CP, CQ, CX, DX, KP, RX, rad_ref,
    ins, us, ur, ts, tr, qs, qr, tps, tpr, txs, txr, cps, cpr, cxs, cxr, dxs, dxr, rs, rr,
):
    z = lax.axis_index("rows")
    f = lax.axis_index("feat")
    core = lax.rem(f, 2)
    chip = lax.div(f, 2)
    n, w = x_ref.shape
    h = n // 2
    rc = n // C
    not_low = z > 0
    not_high = z < R - 1

    bar = pltpu.get_barrier_semaphore()
    for p in range(1, F):
        pl.semaphore_signal(
            bar, inc=1, device_id={"feat": lax.rem(f + p, F)}, device_id_type=MESH
        )

    @pl.when(not_low)
    def _():
        pl.semaphore_signal(bar, inc=1, device_id={"rows": z - 1}, device_id_type=MESH)

    @pl.when(not_high)
    def _():
        pl.semaphore_signal(bar, inc=1, device_id={"rows": z + 1}, device_id_type=MESH)

    x_in = pltpu.make_async_copy(x_hbm, x_ref, ins.at[0])
    t_in = pltpu.make_async_copy(t_hbm, t_ref, ins.at[1])
    x_in.start()
    t_in.start()

    eye = lax.broadcasted_iota(jnp.int32, (n, n), 0) == lax.broadcasted_iota(
        jnp.int32, (n, n), 1
    )

    def to_row(column):
        return jnp.sum(jnp.where(eye, column, 0.0), axis=0, keepdims=True)

    def to_column(row):
        return jnp.sum(jnp.where(eye, row, 0.0), axis=1, keepdims=True)

    x_in.wait()
    x = x_ref[...]
    SQ[f] = jnp.broadcast_to(to_row(jnp.sum(x * x, axis=1, keepdims=True)), (8, n))
    t_in.wait()
    T[z] = t_ref[...]
    pl.semaphore_wait(
        bar, F - 1 + not_low.astype(jnp.int32) + not_high.astype(jnp.int32)
    )

    def remote(src, dst, send, recv, device):
        return pltpu.make_async_remote_copy(
            src_ref=src, dst_ref=dst, send_sem=send, recv_sem=recv,
            device_id=device, device_id_type=MESH,
        )

    def across(entry, index, send, recv, p, mine):
        ref = entry(f if mine else lax.rem(f + F - p, F))
        return remote(
            ref, ref, send.at[index + (p - 1,)], recv.at[index + (p - 1,)],
            {"feat": lax.rem(f + p, F)},
        )

    def spread(entry, index, send, recv):
        for p in range(1, F):
            across(entry, index, send, recv, p, True).start()

    def collect(entry, index, send, recv):
        for p in range(1, F):
            across(entry, index, send, recv, p, False).wait_recv()

    def drained(entry, index, send, recv):
        for p in range(1, F):
            across(entry, index, send, recv, p, True).wait_send()

    def halves(buf, src):
        return lambda g: buf.at[lax.div(g, 2), src, lax.rem(g, 2)]

    def sibling(part, other, src, send, recv):
        return remote(
            part.at[src, 1 - core], other.at[src], send.at[src], recv.at[src],
            {"feat": f + 1 - 2 * core},
        )

    def along(buf, d, src, place, index, send, recv):
        ref = buf.at[(src,) + place]
        target = lax.rem(z + (1 if d == 0 else R - 1), R)
        return remote(
            ref, ref, send.at[(d,) + index], recv.at[(d,) + index], {"rows": target}
        )

    def sends(d, k):
        if d == 0:
            return jnp.logical_and(z - k >= 0, not_high), z - k
        return jnp.logical_and(z + k <= R - 1, not_low), z + k

    def arrives(d, k):
        if d == 0:
            return z - 1 - k >= 0, z - 1 - k
        return z + 1 + k <= R - 1, z + 1 + k

    def each(k, act):
        for d in range(2):
            here, src = arrives(d, k)

            @pl.when(here)
            def _(d=d, src=src):
                act(d, src)

    def t_copy(d, k, src):
        return along(T, d, src, (), (k,), ts, tr)

    def u_copy(d, k, c, src):
        return along(U, d, src, (c,), (k, c), us, ur)

    squares_of = lambda g: SQ.at[g]
    spread(squares_of, (), qs, qr)
    for d in range(2):
        here, src = sends(d, 0)

        @pl.when(here)
        def _(d=d, src=src):
            t_copy(d, 0, src).start()

    collect(squares_of, (), qs, qr)
    squares = SQ[0]
    for g in range(1, F):
        squares = squares + SQ[g]
    scaling = to_column(lax.rsqrt(squares[:1] + EPSILON))
    U[z] = (x_ref[...] * scaling).astype(BF16).reshape(C, rc, w)
    for c in range(C):
        for d in range(2):
            here, src = sends(d, 0)

            @pl.when(here)
            def _(d=d, c=c, src=src):
                u_copy(d, 0, c, src).start()

    def teach(src):
        TP[src] = lax.dot_general(
            T[src], t_ref[...], LAST, preferred_element_type=F32
        ).astype(BF16).reshape(2, h, n)
        sibling(TP, TQ, src, tps, tpr).start()

    def teach_on(src):
        sibling(TP, TQ, src, tps, tpr).wait_recv()
        TX[chip, src, core] = (TP[src, core].astype(F32) + TQ[src].astype(F32)).astype(BF16)
        spread(halves(TX, src), (src,), txs, txr)

    def gram(src, c):
        return lax.dot_general(
            U[src, c], U[z].reshape(n, w), LAST, preferred_element_type=F32
        )

    def study(src, c):
        cosine = gram(src, c)
        KP[src, c] = cosine
        teacher = lax.dot_general(
            T[src].reshape(C, rc, -1)[c], t_ref[...], LAST, preferred_element_type=F32
        )
        CP[src, c] = (cosine - teacher).astype(BF16)
        if c == C - 1:
            sibling(CP, CQ, src, cps, cpr).start()

    def study_on(src):
        sibling(CP, CQ, src, cps, cpr).wait_recv()
        CX[chip, src, core] = (CP[src, core].astype(F32) + CQ[src].astype(F32)).astype(BF16)
        spread(halves(CX, src), (src,), cxs, cxr)

    def direct_of(c):
        return lambda g: DX.at[g, c]

    def study_direct(src, c):
        DX[f, c] = gram(src, c).astype(BF16)
        spread(direct_of(c), (c,), dxs, dxr)

    radial_of = lambda g: RX.at[g]

    def finish(src, first=False, direct=False):
        if direct:
            collect(halves(TX, src), (src,), txs, txr)
            teacher = TX[0, src].astype(F32) + TX[1, src].astype(F32)
            for c in range(C):
                collect(direct_of(c), (c,), dxs, dxr)
            cosine = DX[0].astype(F32)
            for g in range(1, F):
                cosine = cosine + DX[g].astype(F32)
            cosine = cosine.reshape(n, n)
            differ = cosine - teacher.reshape(n, n)
        else:
            collect(halves(CX, src), (src,), cxs, cxr)
            differ = (CX[0, src].astype(F32) + CX[1, src].astype(F32)).reshape(n, n)
            cosine = KP[src].reshape(n, n)
        half = differ.astype(BF16)
        loss = jnp.sum(differ * differ, axis=0, keepdims=True)
        radial = jnp.sum(half.astype(F32) * cosine, axis=0, keepdims=True)
        pulled = lax.dot_general(
            half, U[src].reshape(n, w), FIRST, preferred_element_type=F32
        )
        if first:
            loss_ref[...] = loss
            RX[f] = jnp.broadcast_to(radial, (8, n))
            rad_ref[...] = jnp.zeros_like(radial)
            g_ref[...] = pulled
        else:
            loss_ref[...] += loss
            if direct:
                rad_ref[...] += radial
            else:
                RX[f] += radial
            g_ref[...] += pulled

    for c in range(C):
        study(z, c)
    study_on(z)

    def t_step(k):
        def act(d, src):
            t_copy(d, k, src).wait_recv()
            if k < R - 2:
                @pl.when(sends(d, k + 1)[0])
                def _():
                    t_copy(d, k + 1, src).start()
            else:
                teach(src)

        each(k, act)

    def u_move(k, c, d, side):
        here, src = arrives(d, k)

        @pl.when(jnp.logical_and(here, side))
        def _():
            u_copy(d, k, c, src).wait_recv()
            if k < R - 2:
                @pl.when(sends(d, k + 1)[0])
                def _():
                    u_copy(d, k + 1, c, src).start()

    def u_step(k, c):
        for d in (1, 0):
            u_move(k, c, d, z < R // 2)
        for d in (0, 1):
            u_move(k, c, d, z >= R // 2)
        each(k, lambda d, src: study(src, c) if k < R - 2 else study_direct(src, c))

    for k in range(R - 1):
        t_step(k)
        if k > 0:
            each(k - 1, lambda d, src: study_on(src))
        u_step(k, 0)
        if k == 0:
            finish(z, first=True)
        else:
            if k == R - 2:
                each(k, lambda d, src: teach_on(src))
            each(k - 1, lambda d, src: finish(src))
        if k == R - 2:
            spread(radial_of, (), rs, rr)
        u_step(k, 1)

    each(R - 2, lambda d, src: finish(src, direct=True))

    collect(radial_of, (), rs, rr)
    for g in range(F):
        rad_ref[...] += RX[g, :1]

    factor = 4.0 * D / (n * R)
    loss_ref[...] = (D / (n * R)) * loss_ref[...]
    radial = to_column(rad_ref[...])
    g_ref[...] = (factor * scaling) * (g_ref[...] - (radial * scaling) * x_ref[...])

    drained(squares_of, (), qs, qr)
    drained(radial_of, (), rs, rr)

    def t_drained(d, src):
        sibling(TP, TQ, src, tps, tpr).wait_send()
        drained(halves(TX, src), (src,), txs, txr)

    def c_drained(d, src):
        sibling(CP, CQ, src, cps, cpr).wait_send()
        drained(halves(CX, src), (src,), cxs, cxr)

    c_drained(0, z)
    for k in range(R - 1):
        if k < R - 2:
            each(k, c_drained)
        else:
            each(k, t_drained)
            each(k, lambda d, src: [drained(direct_of(c), (c,), dxs, dxr) for c in range(C)])
        for d in range(2):
            here, src = sends(d, k)

            @pl.when(here)
            def _(d=d, k=k, src=src):
                t_copy(d, k, src).wait_send()
                for c in range(C):
                    u_copy(d, k, c, src).wait_send()


def fused(R, F, student, teacher):
    n, w = student.shape
    wt = teacher.shape[1]
    C = 2
    h = n // 2
    dma = pltpu.SemaphoreType.DMA
    vmem = pl.BlockSpec(memory_space=pltpu.VMEM)
    hbm = pl.BlockSpec(memory_space=pltpu.HBM)
    loss, grad = pl.pallas_call(
        functools.partial(kernel, R, F, C),
        out_shape=(
            jax.ShapeDtypeStruct((1, n), F32),
            jax.ShapeDtypeStruct((n, w), F32),
        ),
        in_specs=[hbm, hbm],
        out_specs=(vmem, vmem),
        scratch_shapes=[
            pltpu.VMEM((n, w), F32),
            pltpu.VMEM((n, wt), BF16),
            pltpu.VMEM((R, C, n // C, w), BF16),
            pltpu.VMEM((R, n, wt), BF16),
            pltpu.VMEM((F, 8, n), F32),
            pltpu.VMEM((R, 2, h, n), BF16),
            pltpu.VMEM((R, h, n), BF16),
            pltpu.VMEM((2, R, 2, h, n), BF16),
            pltpu.VMEM((R, 2, h, n), BF16),
            pltpu.VMEM((R, h, n), BF16),
            pltpu.VMEM((2, R, 2, h, n), BF16),
            pltpu.VMEM((F, C, n // C, n), BF16),
            pltpu.VMEM((R, C, n // C, n), F32),
            pltpu.VMEM((F, 8, n), F32),
            pltpu.VMEM((1, n), F32),
            dma((2,)),
            dma((2, R - 1, C)), dma((2, R - 1, C)),
            dma((2, R - 1)), dma((2, R - 1)),
            dma((F - 1,)), dma((F - 1,)),
            dma((R,)), dma((R,)), dma((R, F - 1)), dma((R, F - 1)),
            dma((R,)), dma((R,)), dma((R, F - 1)), dma((R, F - 1)),
            dma((C, F - 1)), dma((C, F - 1)),
            dma((F - 1,)), dma((F - 1,)),
        ],
        compiler_params=pltpu.CompilerParams(
            collective_id=0, has_side_effects=True, vmem_limit_bytes=48 * 2**20
        ),
    )(pltpu.with_memory_space_constraint(student, pltpu.HBM), pltpu.with_memory_space_constraint(teacher, pltpu.HBM))
    return loss.reshape(n), grad


def solution(mesh):
    R, F = mesh.shape["rows"], mesh.shape["feat"]
    body = functools.partial(fused, R, F) if 3 <= R <= ROWS_LIMIT and F == 4 else ring
    in_specs = (P(("groups", "rows"), "feat"), P(("groups", "rows"), "feat"))
    out_specs = (P(("groups", "rows")), P(("groups", "rows"), "feat"))
    return jax.shard_map(
        body, mesh=mesh, in_specs=in_specs, out_specs=out_specs, check_vma=False
    )
```

```python
import functools

import jax
import jax.numpy as jnp
from jax import lax
from jax.experimental import pallas as pl
from jax.experimental.pallas import tpu as pltpu
from jax.sharding import PartitionSpec as P

D = 4096
EPSILON = 1e-06
ROWS_LIMIT = 8
LAST = (((1,), (1,)), ((), ()))
FIRST = (((0,), (0,)), ((), ()))
F32 = jnp.float32
BF16 = jnp.bfloat16
MESH = pl.DeviceIdType.MESH


def shifted(block, axis, distance):
    devices = range(lax.axis_size(axis))
    route = [((i - distance) % len(devices), i) for i in devices]
    return lax.ppermute(block, axis, route)


def ring(student, teacher):
    cycle = lax.axis_size("rows")
    rows_here = student.shape[0]
    width = student.shape[1]
    embeds = rows_here * cycle
    squares = lax.psum(jnp.sum(student * student, axis=1), "feat")
    scaling = lax.rsqrt(squares + EPSILON)
    unit = student * scaling[:, None]
    unit_half = unit.astype(BF16)
    packed = jnp.concatenate([unit_half, teacher], axis=1)

    def absorb(carry, visitor):
        losses, pulled = carry
        other_unit = visitor[:, :width]
        other_teacher = visitor[:, width:]
        student_term = lax.dot_general(
            unit_half, other_unit, LAST, preferred_element_type=F32
        )
        teacher_term = lax.dot_general(
            teacher, other_teacher, LAST, preferred_element_type=F32
        )
        differ = lax.psum((student_term - teacher_term).astype(BF16), "feat").astype(F32)
        losses = losses + jnp.sum(differ * differ, axis=1)
        pulled = pulled + jnp.dot(
            differ.astype(BF16), other_unit, preferred_element_type=F32
        )
        return (losses, pulled)

    carry = (jnp.zeros((rows_here,), F32), jnp.zeros((rows_here, width), F32))
    carry = absorb(carry, packed)

    def turn(step, state):
        inner, visitor = state
        visitor = shifted(visitor, "rows", 1)
        return (absorb(inner, visitor), visitor)

    carry, visitor = lax.fori_loop(0, cycle - 1, turn, (carry, packed))
    losses, pulled = carry
    radial = lax.psum(jnp.sum(pulled * unit, axis=1), "feat")
    factor = 4.0 * D / embeds
    student_grad = factor * scaling[:, None] * (pulled - radial[:, None] * unit)
    return (D / embeds * losses, student_grad)


def kernel(
    R, F, C, x_hbm, t_hbm, loss_ref, g_ref,
    x_ref, t_ref, U, T, SQ, TP, TQ, TX, CP, CQ, CX, DX, KP, RX, rad_ref,
    ins, us, ur, ts, tr, qs, qr, tps, tpr, txs, txr, cps, cpr, cxs, cxr, dxs, dxr, rs, rr,
):
    z = lax.axis_index("rows")
    f = lax.axis_index("feat")
    core = lax.rem(f, 2)
    chip = lax.div(f, 2)
    n, w = x_ref.shape
    h = n // 2
    rc = n // C
    not_low = z > 0
    not_high = z < R - 1

    bar = pltpu.get_barrier_semaphore()
    for p in range(1, F):
        pl.semaphore_signal(
            bar, inc=1, device_id={"feat": lax.rem(f + p, F)}, device_id_type=MESH
        )

    @pl.when(not_low)
    def _():
        pl.semaphore_signal(bar, inc=1, device_id={"rows": z - 1}, device_id_type=MESH)

    @pl.when(not_high)
    def _():
        pl.semaphore_signal(bar, inc=1, device_id={"rows": z + 1}, device_id_type=MESH)

    x_in = pltpu.make_async_copy(x_hbm, x_ref, ins.at[0])
    t_in = pltpu.make_async_copy(t_hbm, t_ref, ins.at[1])
    t_in.start()
    x_in.start()

    eye = lax.broadcasted_iota(jnp.int32, (n, n), 0) == lax.broadcasted_iota(
        jnp.int32, (n, n), 1
    )

    def to_row(column):
        return jnp.sum(jnp.where(eye, column, 0.0), axis=0, keepdims=True)

    def to_column(row):
        return jnp.sum(jnp.where(eye, row, 0.0), axis=1, keepdims=True)

    t_in.wait()
    T[z] = t_ref[...]
    pl.semaphore_wait(
        bar, F - 1 + not_low.astype(jnp.int32) + not_high.astype(jnp.int32)
    )

    def remote(src, dst, send, recv, device):
        return pltpu.make_async_remote_copy(
            src_ref=src, dst_ref=dst, send_sem=send, recv_sem=recv,
            device_id=device, device_id_type=MESH,
        )

    def across(entry, index, send, recv, p, mine):
        ref = entry(f if mine else lax.rem(f + F - p, F))
        return remote(
            ref, ref, send.at[index + (p - 1,)], recv.at[index + (p - 1,)],
            {"feat": lax.rem(f + p, F)},
        )

    def spread(entry, index, send, recv):
        for p in range(1, F):
            across(entry, index, send, recv, p, True).start()

    def collect(entry, index, send, recv):
        for p in range(1, F):
            across(entry, index, send, recv, p, False).wait_recv()

    def drained(entry, index, send, recv):
        for p in range(1, F):
            across(entry, index, send, recv, p, True).wait_send()

    def halves(buf, src):
        return lambda g: buf.at[lax.div(g, 2), src, lax.rem(g, 2)]

    def sibling(part, other, src, send, recv):
        return remote(
            part.at[src, 1 - core], other.at[src], send.at[src], recv.at[src],
            {"feat": f + 1 - 2 * core},
        )

    def along(buf, d, src, place, index, send, recv):
        ref = buf.at[(src,) + place]
        target = lax.rem(z + (1 if d == 0 else R - 1), R)
        return remote(
            ref, ref, send.at[(d,) + index], recv.at[(d,) + index], {"rows": target}
        )

    def sends(d, k):
        if d == 0:
            return jnp.logical_and(z - k >= 0, not_high), z - k
        return jnp.logical_and(z + k <= R - 1, not_low), z + k

    def arrives(d, k):
        if d == 0:
            return z - 1 - k >= 0, z - 1 - k
        return z + 1 + k <= R - 1, z + 1 + k

    def each(k, act):
        for d in range(2):
            here, src = arrives(d, k)

            @pl.when(here)
            def _(d=d, src=src):
                act(d, src)

    def t_copy(d, k, src):
        return along(T, d, src, (), (k,), ts, tr)

    def u_copy(d, k, c, src):
        return along(U, d, src, (c,), (k, c), us, ur)

    for d in range(2):
        here, src = sends(d, 0)

        @pl.when(here)
        def _(d=d, src=src):
            t_copy(d, 0, src).start()

    x_in.wait()
    x = x_ref[...]
    SQ[f] = jnp.broadcast_to(to_row(jnp.sum(x * x, axis=1, keepdims=True)), (8, n))
    squares_of = lambda g: SQ.at[g]
    spread(squares_of, (), qs, qr)
    collect(squares_of, (), qs, qr)
    squares = SQ[0]
    for g in range(1, F):
        squares = squares + SQ[g]
    scaling = to_column(lax.rsqrt(squares[:1] + EPSILON))
    U[z] = (x_ref[...] * scaling).astype(BF16).reshape(C, rc, w)
    for c in range(C):
        for d in range(2):
            here, src = sends(d, 0)

            @pl.when(here)
            def _(d=d, c=c, src=src):
                u_copy(d, 0, c, src).start()

    def teach(src):
        TP[src] = lax.dot_general(
            T[src], t_ref[...], LAST, preferred_element_type=F32
        ).astype(BF16).reshape(2, h, n)
        sibling(TP, TQ, src, tps, tpr).start()

    def teach_on(src):
        sibling(TP, TQ, src, tps, tpr).wait_recv()
        TX[chip, src, core] = (TP[src, core].astype(F32) + TQ[src].astype(F32)).astype(BF16)
        spread(halves(TX, src), (src,), txs, txr)

    def gram(src, c):
        return lax.dot_general(
            U[src, c], U[z].reshape(n, w), LAST, preferred_element_type=F32
        )

    def study(src, c):
        cosine = gram(src, c)
        KP[src, c] = cosine
        teacher = lax.dot_general(
            T[src].reshape(C, rc, -1)[c], t_ref[...], LAST, preferred_element_type=F32
        )
        CP[src, c] = (cosine - teacher).astype(BF16)
        if c == C - 1:
            sibling(CP, CQ, src, cps, cpr).start()

    def study_on(src):
        sibling(CP, CQ, src, cps, cpr).wait_recv()
        CX[chip, src, core] = (CP[src, core].astype(F32) + CQ[src].astype(F32)).astype(BF16)
        spread(halves(CX, src), (src,), cxs, cxr)

    def direct_of(c):
        return lambda g: DX.at[g, c]

    def study_direct(src, c):
        DX[f, c] = gram(src, c).astype(BF16)
        spread(direct_of(c), (c,), dxs, dxr)

    radial_of = lambda g: RX.at[g]

    def finish(src, first=False, direct=False):
        if direct:
            collect(halves(TX, src), (src,), txs, txr)
            teacher = TX[0, src].astype(F32) + TX[1, src].astype(F32)
            for c in range(C):
                collect(direct_of(c), (c,), dxs, dxr)
            cosine = DX[0].astype(F32)
            for g in range(1, F):
                cosine = cosine + DX[g].astype(F32)
            cosine = cosine.reshape(n, n)
            differ = cosine - teacher.reshape(n, n)
        else:
            collect(halves(CX, src), (src,), cxs, cxr)
            differ = (CX[0, src].astype(F32) + CX[1, src].astype(F32)).reshape(n, n)
            cosine = KP[src].reshape(n, n)
        half = differ.astype(BF16)
        loss = jnp.sum(differ * differ, axis=0, keepdims=True)
        radial = jnp.sum(half.astype(F32) * cosine, axis=0, keepdims=True)
        pulled = lax.dot_general(
            half, U[src].reshape(n, w), FIRST, preferred_element_type=F32
        )
        if first:
            loss_ref[...] = loss
            RX[f] = jnp.broadcast_to(radial, (8, n))
            rad_ref[...] = jnp.zeros_like(radial)
            g_ref[...] = pulled
        else:
            loss_ref[...] += loss
            if direct:
                rad_ref[...] += radial
            else:
                RX[f] += radial
            g_ref[...] += pulled

    for c in range(C):
        study(z, c)
    study_on(z)

    def t_step(k):
        def act(d, src):
            t_copy(d, k, src).wait_recv()
            if k < R - 2:
                @pl.when(sends(d, k + 1)[0])
                def _():
                    t_copy(d, k + 1, src).start()
            else:
                teach(src)

        each(k, act)

    def u_move(k, c, d, side):
        here, src = arrives(d, k)

        @pl.when(jnp.logical_and(here, side))
        def _():
            u_copy(d, k, c, src).wait_recv()
            if k < R - 2:
                @pl.when(sends(d, k + 1)[0])
                def _():
                    u_copy(d, k + 1, c, src).start()

    def u_step(k, c):
        for d in (1, 0):
            u_move(k, c, d, z < R // 2)
        for d in (0, 1):
            u_move(k, c, d, z >= R // 2)
        each(k, lambda d, src: study(src, c) if k < R - 2 else study_direct(src, c))

    for k in range(R - 1):
        t_step(k)
        if k > 0:
            each(k - 1, lambda d, src: study_on(src))
        u_step(k, 0)
        if k == 0:
            finish(z, first=True)
        else:
            if k == R - 2:
                each(k, lambda d, src: teach_on(src))
            each(k - 1, lambda d, src: finish(src))
        if k == R - 2:
            spread(radial_of, (), rs, rr)
        u_step(k, 1)

    each(R - 2, lambda d, src: finish(src, direct=True))

    collect(radial_of, (), rs, rr)
    for g in range(F):
        rad_ref[...] += RX[g, :1]

    factor = 4.0 * D / (n * R)
    loss_ref[...] = (D / (n * R)) * loss_ref[...]
    radial = to_column(rad_ref[...])
    g_ref[...] = (factor * scaling) * (g_ref[...] - (radial * scaling) * x_ref[...])

    drained(squares_of, (), qs, qr)
    drained(radial_of, (), rs, rr)

    def t_drained(d, src):
        sibling(TP, TQ, src, tps, tpr).wait_send()
        drained(halves(TX, src), (src,), txs, txr)

    def c_drained(d, src):
        sibling(CP, CQ, src, cps, cpr).wait_send()
        drained(halves(CX, src), (src,), cxs, cxr)

    c_drained(0, z)
    for k in range(R - 1):
        if k < R - 2:
            each(k, c_drained)
        else:
            each(k, t_drained)
            each(k, lambda d, src: [drained(direct_of(c), (c,), dxs, dxr) for c in range(C)])
        for d in range(2):
            here, src = sends(d, k)

            @pl.when(here)
            def _(d=d, k=k, src=src):
                t_copy(d, k, src).wait_send()
                for c in range(C):
                    u_copy(d, k, c, src).wait_send()


def fused(R, F, student, teacher):
    n, w = student.shape
    wt = teacher.shape[1]
    C = 2
    h = n // 2
    dma = pltpu.SemaphoreType.DMA
    vmem = pl.BlockSpec(memory_space=pltpu.VMEM)
    hbm = pl.BlockSpec(memory_space=pltpu.HBM)
    loss, grad = pl.pallas_call(
        functools.partial(kernel, R, F, C),
        out_shape=(
            jax.ShapeDtypeStruct((1, n), F32),
            jax.ShapeDtypeStruct((n, w), F32),
        ),
        in_specs=[hbm, hbm],
        out_specs=(vmem, vmem),
        scratch_shapes=[
            pltpu.VMEM((n, w), F32),
            pltpu.VMEM((n, wt), BF16),
            pltpu.VMEM((R, C, n // C, w), BF16),
            pltpu.VMEM((R, n, wt), BF16),
            pltpu.VMEM((F, 8, n), F32),
            pltpu.VMEM((R, 2, h, n), BF16),
            pltpu.VMEM((R, h, n), BF16),
            pltpu.VMEM((2, R, 2, h, n), BF16),
            pltpu.VMEM((R, 2, h, n), BF16),
            pltpu.VMEM((R, h, n), BF16),
            pltpu.VMEM((2, R, 2, h, n), BF16),
            pltpu.VMEM((F, C, n // C, n), BF16),
            pltpu.VMEM((R, C, n // C, n), F32),
            pltpu.VMEM((F, 8, n), F32),
            pltpu.VMEM((1, n), F32),
            dma((2,)),
            dma((2, R - 1, C)), dma((2, R - 1, C)),
            dma((2, R - 1)), dma((2, R - 1)),
            dma((F - 1,)), dma((F - 1,)),
            dma((R,)), dma((R,)), dma((R, F - 1)), dma((R, F - 1)),
            dma((R,)), dma((R,)), dma((R, F - 1)), dma((R, F - 1)),
            dma((C, F - 1)), dma((C, F - 1)),
            dma((F - 1,)), dma((F - 1,)),
        ],
        compiler_params=pltpu.CompilerParams(
            collective_id=0, has_side_effects=True, vmem_limit_bytes=48 * 2**20
        ),
    )(pltpu.with_memory_space_constraint(student, pltpu.HBM), pltpu.with_memory_space_constraint(teacher, pltpu.HBM))
    return loss.reshape(n), grad


def solution(mesh):
    R, F = mesh.shape["rows"], mesh.shape["feat"]
    body = functools.partial(fused, R, F) if 3 <= R <= ROWS_LIMIT and F == 4 else ring
    in_specs = (P(("groups", "rows"), "feat"), P(("groups", "rows"), "feat"))
    out_specs = (P(("groups", "rows")), P(("groups", "rows"), "feat"))
    return jax.shard_map(
        body, mesh=mesh, in_specs=in_specs, out_specs=out_specs, check_vma=False
    )
```
